32 devices in a mesh: seq: 16 (over z, y, core), head: 2 (over x).
Axes of the slice: x: 2, y: 2, z: 4, core: 2. Of those that a mesh axis runs over, the one named last changes fastest.
Arguments:
- queries: bfloat16 [8192, 4096], P(('seq', 'head')), may hold values from -64 to 64
- keys: bfloat16 [8192, 1024], P(('seq', 'head')), may hold values from -6 to 6
- values: bfloat16 [8192, 1024], P(('seq', 'head')), may hold values from -6 to 6
- level_bias: float32 [32, 4], P('head'), may hold values from -1 to 2
- anchor_bias: float32 [32], P('head'), may hold values from 1 to 4
- partners: int32 [16, 4], P('seq'), may hold values from 0 to 15, as said below
- anchor_positions: int32 [64], replicated, may hold values from 0 to 8191, as said below
Outputs:
- attended: bfloat16 [8192, 4096], P(('seq', 'head'))
The draws below stay inside these ranges and needn't reach their ends.
Inputs may be any that keep to these rules, and one draw needn't show every extreme that they name: `partners`: row b holds b XOR 2**j once for each j of 0 to 3, in an order drawn for each block. `anchor_positions`: distinct positions.
All inputs are finite; a program needn't handle non-finite values.
Results may differ from the reference program's by a relative error of at most 0.0045.
Values may be sent and summed in bfloat16 or wider, within the bound.
A program may use at most 192 MiB of HBM per device.

```python
import math
import jax
import jax.numpy as jnp
from jax import lax

QH = 32
KVH = 8
HD = 128
TOK_DEV = 512
NGLOB = 64
BLOCKS = 16
LEVELS = 4
TOKENS = 8192


def shared_keys(key):
    base_key = jax.random.fold_in(key, 7)
    drawn = jnp.clip(jax.random.normal(base_key, (TOKENS, KVH * HD), jnp.float32), -6.0, 6.0)
    return drawn


def draw_keys(key, part):
    drawn = shared_keys(key)
    return drawn.astype(jnp.bfloat16)


def draw_queries(key, part):
    noise_key = jax.random.fold_in(key, 13)
    result = jnp.clip(2.0 * jax.random.normal(noise_key, (TOKENS, QH * HD), jnp.float32), -8.0, 8.0)
    return result.astype(jnp.bfloat16)


def draw_partners(key, part):

    def one_block(block):
        order_bits = jax.random.permutation(jax.random.fold_in(key, block), LEVELS)
        return jnp.bitwise_xor(block, jnp.left_shift(1, order_bits)).astype(jnp.int32)
    return jax.vmap(one_block)(jnp.arange(BLOCKS, dtype=jnp.int32))


def draw_anchor_positions(key, part):
    return jax.random.permutation(jax.random.fold_in(key, 5), TOKENS)[:NGLOB].astype(jnp.int32)


def block_levels(stream_key, dims, split, smallest, largest):
    factor_of, own = 1.0, jax.random.fold_in(stream_key, 6)
    for axis_at, shards_of in split:
        draws = jnp.exp(jax.random.uniform(jax.random.fold_in(own, axis_at), (shards_of,), jnp.float32, smallest / len(split), largest / len(split)))
        factor_of = factor_of * jnp.repeat(draws, dims[axis_at] // shards_of).reshape([-1 if axis == axis_at else 1 for axis in range(len(dims))])
    return factor_of


def scatter_about(stream_key, extent, scale, most, split=(), kind=jnp.bfloat16):
    gain = block_levels(stream_key, extent, split, -0.22, 0.18) if split else 1.0
    values = jax.random.normal(stream_key, extent, jnp.float32) * scale * gain
    return jnp.minimum(jnp.maximum(values, -most), most).astype(kind)


def setup_inputs(seed: int = 0) -> dict:
    arg_keys = jax.random.split(jax.random.key(seed), 8)
    queries = draw_queries(jax.random.fold_in(arg_keys[7], 71), 0)
    keys = draw_keys(jax.random.fold_in(arg_keys[7], 71), 0)
    values = scatter_about(arg_keys[2], (TOKENS, KVH * HD), 1.0, 6.0, ((0, 32),))
    level_bias = jnp.clip(-1.0 + 3.0 * jax.random.uniform(arg_keys[3], (QH, LEVELS), jnp.float32) ** block_levels(arg_keys[3], (QH, LEVELS), ((0, 2),), -0.2, 0.2), -1.0, 2.0)
    anchor_bias = jnp.clip(jnp.exp(math.log(4.0) - 1.3862944 * jax.random.uniform(arg_keys[4], (QH,), jnp.float32) ** block_levels(arg_keys[4], (QH,), ((0, 2),), -0.2, 0.2)), 1.0, 4.0)
    partners = draw_partners(jax.random.fold_in(arg_keys[7], 71), 0)
    anchor_positions = draw_anchor_positions(jax.random.fold_in(arg_keys[7], 71), 0)
    return dict(queries=queries, keys=keys, values=values, level_bias=level_bias, anchor_bias=anchor_bias, partners=partners, anchor_positions=anchor_positions)


def reference(queries, keys, values, level_bias, anchor_bias, partners, anchor_positions):
    group_size = QH // KVH
    score_scale = HD ** -0.5
    anchor_keys = keys[anchor_positions]
    anchor_vals = values[anchor_positions]
    pieces = [jnp.zeros((QH, TOK_DEV), jnp.float32)]
    for level in range(LEVELS):
        pieces.append(jnp.broadcast_to(level_bias[:, level:level + 1], (QH, TOK_DEV)))
    pieces.append(jnp.broadcast_to(anchor_bias[:, None], (QH, NGLOB)))
    key_bias = jnp.concatenate(pieces, axis=1).reshape(KVH, group_size, -1)

    def attend_block(block):
        start = (block * TOK_DEV).astype(jnp.int32)
        query_heads = lax.dynamic_slice_in_dim(queries, start, TOK_DEV, 0).reshape(TOK_DEV, KVH, group_size, HD)
        key_list = [lax.dynamic_slice_in_dim(keys, start, TOK_DEV, 0)]
        value_list = [lax.dynamic_slice_in_dim(values, start, TOK_DEV, 0)]
        for level in range(LEVELS):
            other = (partners[block, level] * TOK_DEV).astype(jnp.int32)
            key_list.append(lax.dynamic_slice_in_dim(keys, other, TOK_DEV, 0))
            value_list.append(lax.dynamic_slice_in_dim(values, other, TOK_DEV, 0))
        key_rows = jnp.concatenate(key_list + [anchor_keys], axis=0).reshape(-1, KVH, HD)
        value_rows = jnp.concatenate(value_list + [anchor_vals], axis=0).reshape(-1, KVH, HD)
        scores = jnp.einsum("tkgd,skd->kgts", query_heads.astype(jnp.float32), key_rows.astype(jnp.float32))
        scores = scores * score_scale + key_bias[:, :, None, :]
        row_max = jnp.max(scores, axis=-1, keepdims=True)
        weights = jnp.exp(scores - row_max)
        denominator = jnp.sum(weights, axis=-1)
        rounded = lax.optimization_barrier(weights.astype(jnp.bfloat16)).astype(jnp.float32)
        numerator = jnp.einsum("kgts,skd->kgtd", rounded, value_rows.astype(jnp.float32))
        result = numerator / denominator[..., None]
        return result.transpose(2, 0, 1, 3).reshape(TOK_DEV, QH * HD).astype(jnp.bfloat16)

    blocks_out = lax.map(attend_block, jnp.arange(BLOCKS, dtype=jnp.int32))
    return blocks_out.reshape(TOKENS, QH * HD)
```

```python
import functools

import jax
import jax.numpy as jnp
from jax import lax
from jax.experimental import pallas as pl
from jax.experimental.pallas import tpu as pltpu
from jax.sharding import PartitionSpec as P

HD = 128

LOG2E = 1.4426950408889634

def attend(query, key_parts, value_parts, biases, scale):
    scores = [
        lax.dot_general(query, k, (((1,), (1,)), ((), ())), preferred_element_type=jnp.float32)
        for k in key_parts
    ]
    row_max = None
    for s, b in zip(scores, biases):
        top = jnp.max(s, axis=1, keepdims=True) * scale + b
        row_max = top if row_max is None else jnp.maximum(row_max, top)
    total = None
    acc = None
    for s, v, b in zip(scores, value_parts, biases):
        p = jnp.exp2(s * scale + (b - row_max))
        part = jnp.sum(p, axis=1, keepdims=True)
        out = jnp.dot(p.astype(jnp.bfloat16), v, preferred_element_type=jnp.float32)
        total = part if total is None else total + part
        acc = out if acc is None else acc + out
    return acc / total

def kernel(levels, group, head_dim, tile, unroll, bias_ref, q_ref, ko, vo, *rest):
    kp = rest[:levels]; vp = rest[levels:2*levels]; ka, va, o_ref = rest[2*levels:]
    j = pl.program_id(0)
    scale = head_dim ** -0.5 * LOG2E
    ks = [ko] + list(kp) + [ka]; vs = [vo] + list(vp) + [va]
    rows = q_ref.shape[0]
    def step(i, _):
      for u in range(unroll):
        r = pl.multiple_of((i * unroll + u) * tile, tile)
        for g in range(group):
            q = q_ref[pl.ds(r, tile), g*head_dim:(g+1)*head_dim]
            bs = [bias_ref[j*group+g, n] for n in range(levels+2)]
            o = attend(q, [k[...] for k in ks], [v[...] for v in vs], bs, scale)
            o_ref[pl.ds(r, tile), g*head_dim:(g+1)*head_dim] = o.astype(o_ref.dtype)
      return 0
    lax.fori_loop(0, rows // (tile*unroll), step, 0)

def flash(q, ko, vo, kps, vps, ka, va, bias, kv_local, group, head_dim, tile, unroll):
    T = q.shape[0]
    levels = len(kps)
    col = lambda r, w: pl.BlockSpec((r, w), lambda j: (0, j))
    A = ka.shape[0]
    return pl.pallas_call(
        functools.partial(kernel, levels, group, head_dim, tile, unroll),
        grid=(kv_local,),
        in_specs=[pl.BlockSpec(memory_space=pltpu.SMEM), col(T, group*head_dim)] + [col(T, head_dim)]*(2+2*levels) + [col(A, head_dim)]*2,
        out_specs=col(T, group*head_dim),
        out_shape=jax.ShapeDtypeStruct(q.shape, q.dtype),
        name="attend",
    )(bias, q, ko, vo, *kps, *vps, ka, va)


def partner_2(value, axis, stride):
    return lax.ppermute(value, axis, [(i, i ^ 1 << stride) for i in range(lax.axis_size(axis))])


def on_device(queries, keys, values, level_bias, anchor_bias, partners, anchor_positions):
    key_rows = lax.all_to_all(keys, "head", split_axis=1, concat_axis=0, tiled=True)
    value_rows = lax.all_to_all(values, "head", split_axis=1, concat_axis=0, tiled=True)
    query_rows = lax.all_to_all(queries, "head", split_axis=1, concat_axis=0, tiled=True)
    block_rows = query_rows.shape[0]
    kv_local = key_rows.shape[1] // HD
    group_size = level_bias.shape[0] // kv_local
    block_index = lax.axis_index("seq")
    level_count = lax.axis_size("seq").bit_length() - 1
    token_index = block_index * block_rows + jnp.arange(block_rows, dtype=jnp.int32)
    selector = (anchor_positions[:, None] == token_index[None, :]).astype(jnp.bfloat16)
    carried_keys = jnp.dot(selector, key_rows, preferred_element_type=jnp.float32).astype(jnp.bfloat16)
    carried_vals = jnp.dot(selector, value_rows, preferred_element_type=jnp.float32).astype(jnp.bfloat16)
    key_parts, value_parts, biases = [], [], [jnp.zeros_like(anchor_bias)]
    for bit_level in range(level_count):
        pk, pv = partner_2((key_rows, value_rows), "seq", bit_level)
        more_keys, more_vals = partner_2((carried_keys, carried_vals), "seq", bit_level)
        carried_keys = carried_keys + more_keys
        carried_vals = carried_vals + more_vals
        partner = jnp.bitwise_xor(block_index, 1 << bit_level)
        chosen = (partners[0] == partner).astype(jnp.float32)
        key_parts.append(pk)
        value_parts.append(pv)
        biases.append(jnp.sum(level_bias * chosen[None, :], axis=1))
    biases.append(anchor_bias)
    bias = jnp.stack(biases, axis=1) * LOG2E
    tile = min(256, block_rows)
    result = flash(query_rows, key_rows, value_rows, key_parts, value_parts,
                   carried_keys, carried_vals, bias, kv_local, group_size, HD, tile, 1)
    return lax.all_to_all(result, "head", split_axis=0, concat_axis=1, tiled=True)


def solution(mesh):
    in_specs = (
        P(("seq", "head"), None),
        P(("seq", "head"), None),
        P(("seq", "head"), None),
        P("head", None),
        P("head"),
        P("seq", None),
        P(),
    )
    out_specs = P(("seq", "head"), None)
    return jax.shard_map(
        on_device, mesh=mesh, in_specs=in_specs, out_specs=out_specs, check_vma=False
    )
```

```python
import functools

import jax
import jax.numpy as jnp
from jax import lax
from jax.experimental import pallas as pl
from jax.experimental.pallas import tpu as pltpu
from jax.sharding import PartitionSpec as P

HD = 128
LOG2E = 1.4426950408889634


def attend(query, key_parts, value_parts, biases, scale):
    scores = [
        lax.dot_general(query, k, (((1,), (1,)), ((), ())), preferred_element_type=jnp.float32)
        for k in key_parts
    ]
    row_max = None
    for s, b in zip(scores, biases):
        top = jnp.max(s, axis=1, keepdims=True) * scale + b
        row_max = top if row_max is None else jnp.maximum(row_max, top)
    total = None
    acc = None
    for s, v, b in zip(scores, value_parts, biases):
        p = jnp.exp2(s * scale + (b - row_max))
        part = jnp.sum(p, axis=1, keepdims=True)
        out = jnp.dot(p.astype(jnp.bfloat16), v, preferred_element_type=jnp.float32)
        total = part if total is None else total + part
        acc = out if acc is None else acc + out
    return acc / total


def kernel(
    heads, levels, kv_local, group,
    bias_ref, sel_ref, keys_ref, values_ref, queries_ref, out_ref,
    blocks, qbuf, obuf, part, part_in, carry, carry_in,
    part_send, part_recv, carry_send, carry_recv,
    own_sem, x_send, x_recv, own_q_sem, q_send, q_recv,
    lv_send, lv_recv, own_o_sem, o_send, o_recv,
):
    me = lax.axis_index("head")
    seat = lax.axis_index("seq")
    t = keys_ref.shape[0]
    wide = group * HD
    scale = HD ** -0.5 * LOG2E
    mesh_id = pl.DeviceIdType.MESH

    def peer(d):
        return lax.rem(me + d, heads)

    def partner(l):
        bit = lax.rem(lax.div(seat, 1 << l), 2)
        return seat + (1 - 2 * bit) * (1 << l)

    barrier = pltpu.get_barrier_semaphore()
    for d in range(1, heads):
        pl.semaphore_signal(barrier, inc=1, device_id={"head": peer(d)}, device_id_type=mesh_id)
    for l in range(levels):
        pl.semaphore_signal(barrier, inc=1, device_id={"seq": partner(l)}, device_id_type=mesh_id)

    def cols(owner, j, width):
        return pl.ds(pl.multiple_of((owner * kv_local + j) * width, width), width)

    def rows(owner):
        return pl.ds(pl.multiple_of(owner * t, t), t)

    def own_copy(j, c):
        src = (keys_ref, values_ref)[c]
        return pltpu.make_async_copy(
            src.at[:, cols(me, j, HD)], blocks.at[0, j, c, rows(me)], own_sem.at[j, c])

    def own_q(j):
        return pltpu.make_async_copy(
            queries_ref.at[:, cols(me, j, wide)], qbuf.at[j, rows(me)], own_q_sem.at[j])

    def send_kv(j, c, d):
        src = (keys_ref, values_ref)[c]
        return pltpu.make_async_remote_copy(
            src_ref=src.at[:, cols(peer(d), j, HD)], dst_ref=blocks.at[0, j, c, rows(me)],
            send_sem=x_send.at[j, c, d], recv_sem=x_recv.at[j, c, d],
            device_id={"head": peer(d)}, device_id_type=mesh_id)

    def came_kv(j, c, d):
        src = (keys_ref, values_ref)[c]
        return pltpu.make_async_remote_copy(
            src_ref=src.at[:, cols(me, j, HD)], dst_ref=blocks.at[0, j, c, rows(peer(heads - d))],
            send_sem=x_send.at[j, c, d], recv_sem=x_recv.at[j, c, d],
            device_id={"head": peer(d)}, device_id_type=mesh_id)

    def send_q(j, d):
        return pltpu.make_async_remote_copy(
            src_ref=queries_ref.at[:, cols(peer(d), j, wide)], dst_ref=qbuf.at[j, rows(me)],
            send_sem=q_send.at[j, d], recv_sem=q_recv.at[j, d],
            device_id={"head": peer(d)}, device_id_type=mesh_id)

    def came_q(j, d):
        return pltpu.make_async_remote_copy(
            src_ref=queries_ref.at[:, cols(me, j, wide)], dst_ref=qbuf.at[j, rows(peer(heads - d))],
            send_sem=q_send.at[j, d], recv_sem=q_recv.at[j, d],
            device_id={"head": peer(d)}, device_id_type=mesh_id)

    def send_level(j, l):
        return pltpu.make_async_remote_copy(
            src_ref=blocks.at[0, j], dst_ref=blocks.at[l + 1, j],
            send_sem=lv_send.at[j, l], recv_sem=lv_recv.at[j, l],
            device_id={"seq": partner(l)}, device_id_type=mesh_id)

    def send_part(d):
        return pltpu.make_async_remote_copy(
            src_ref=part.at[d], dst_ref=part_in.at[d],
            send_sem=part_send.at[d], recv_sem=part_recv.at[d],
            device_id={"head": peer(d)}, device_id_type=mesh_id)

    def send_carry(l):
        return pltpu.make_async_remote_copy(
            src_ref=carry.at[l + 1], dst_ref=carry_in.at[l],
            send_sem=carry_send.at[l], recv_sem=carry_recv.at[l],
            device_id={"seq": partner(l)}, device_id_type=mesh_id)

    def send_out(j, d):
        return pltpu.make_async_remote_copy(
            src_ref=obuf.at[j, d], dst_ref=out_ref.at[:, cols(me, j, wide)],
            send_sem=o_send.at[j, d], recv_sem=o_recv.at[j, d],
            device_id={"head": peer(d)}, device_id_type=mesh_id)

    def came_out(j, d):
        return pltpu.make_async_remote_copy(
            src_ref=obuf.at[j, d], dst_ref=out_ref.at[:, cols(peer(heads - d), j, wide)],
            send_sem=o_send.at[j, d], recv_sem=o_recv.at[j, d],
            device_id={"head": peer(d)}, device_id_type=mesh_id)

    def own_out(j):
        return pltpu.make_async_copy(
            obuf.at[j, 0], out_ref.at[:, cols(me, j, wide)], own_o_sem.at[j])

    for j in range(kv_local):
        for c in range(2):
            own_copy(j, c).start()
        own_q(j).start()
    for d in range(heads):
        for j in range(kv_local):
            for c in range(2):
                src = (keys_ref, values_ref)[c]
                part[d, j, c] = jnp.dot(
                    sel_ref[...], src[:, cols(peer(d), j, HD)], preferred_element_type=jnp.float32
                ).astype(jnp.bfloat16)
    pl.semaphore_wait(barrier, heads - 1 + levels)
    for d in range(1, heads):
        send_part(d).start()
    for j in range(kv_local):
        for d in range(1, heads):
            for c in range(2):
                send_kv(j, c, d).start()
    for j in range(kv_local):
        for d in range(1, heads):
            send_q(j, d).start()

    def forward(j):
        for c in range(2):
            own_copy(j, c).wait()
            for d in range(1, heads):
                came_kv(j, c, d).wait_recv()
        for l in reversed(range(levels)):
            send_level(j, l).start()

    held = part[0].astype(jnp.float32)
    for d in range(1, heads):
        send_part(d).wait_recv()
        held = held + part_in[d].astype(jnp.float32)
    carry[levels] = held.astype(jnp.bfloat16)
    sent = 0
    for l in reversed(range(levels)):
        send_carry(l).start()
        if sent < kv_local:
            forward(sent)
            sent += 1
        send_carry(l).wait_recv()
        carry[l] = (carry[l + 1].astype(jnp.float32) + carry_in[l].astype(jnp.float32)).astype(
            jnp.bfloat16)
    for j in range(sent, kv_local):
        forward(j)

    def one(step, _):
        j = lax.div(step, heads)
        turn = lax.rem(step, heads)

        @pl.when(turn == 0)
        def _():
            own_q(j).wait()
            for d in range(1, heads):
                came_q(j, d).wait_recv()
            for l in range(levels):
                send_level(j, l).wait_recv()

        d = lax.rem(turn + 1, heads)
        here = rows(peer(d))
        for g in range(group):
            result = attend(
                qbuf[j, here, g * HD:(g + 1) * HD],
                [blocks[n, j, 0] for n in range(levels + 1)] + [carry[0, j, 0]],
                [blocks[n, j, 1] for n in range(levels + 1)] + [carry[0, j, 1]],
                [bias_ref[j * group + g, n] for n in range(levels + 2)],
                scale,
            )
            obuf[j, d, :, g * HD:(g + 1) * HD] = result.astype(jnp.bfloat16)

        @pl.when(turn < heads - 1)
        def _():
            send_out(j, d).start()

        @pl.when(turn == heads - 1)
        def _():
            own_out(j).start()

        return 0

    lax.fori_loop(0, kv_local * heads, one, 0)

    for d in range(1, heads):
        send_part(d).wait_send()
    for l in range(levels):
        send_carry(l).wait_send()
    for j in range(kv_local):
        own_out(j).wait()
        for l in range(levels):
            send_level(j, l).wait_send()
        for d in range(1, heads):
            for c in range(2):
                send_kv(j, c, d).wait_send()
            send_q(j, d).wait_send()
            send_out(j, d).wait_send()
            came_out(j, d).wait_recv()


def on_device(queries, keys, values, level_bias, anchor_bias, partners, anchor_positions):
    t = queries.shape[0]
    heads = lax.axis_size("head")
    levels = lax.axis_size("seq").bit_length() - 1
    kv_local = keys.shape[1] // HD // heads
    group = level_bias.shape[0] // kv_local
    anchors = anchor_positions.shape[0]
    block_index = lax.axis_index("seq")
    first = (block_index * heads + lax.axis_index("head")) * t
    token_index = first + jnp.arange(t, dtype=jnp.int32)
    selector = (anchor_positions[:, None] == token_index[None, :]).astype(jnp.bfloat16)
    biases = [jnp.zeros_like(anchor_bias)]
    for l in range(levels):
        chosen = (partners[0] == jnp.bitwise_xor(block_index, 1 << l)).astype(jnp.float32)
        biases.append(jnp.sum(level_bias * chosen[None, :], axis=1))
    biases.append(anchor_bias)
    bias = jnp.stack(biases, axis=1) * LOG2E
    vmem = pl.BlockSpec(memory_space=pltpu.VMEM)
    dma = pltpu.SemaphoreType.DMA
    anchor_shape = (kv_local, 2, anchors, HD)
    bf16 = jnp.bfloat16
    return pl.pallas_call(
        functools.partial(kernel, heads, levels, kv_local, group),
        in_specs=[pl.BlockSpec(memory_space=pltpu.SMEM), vmem, vmem, vmem,
                  pl.BlockSpec(memory_space=pl.ANY)],
        out_specs=pl.BlockSpec(memory_space=pl.ANY),
        out_shape=jax.ShapeDtypeStruct(queries.shape, queries.dtype),
        scratch_shapes=[
            pltpu.VMEM((levels + 1, kv_local, 2, t * heads, HD), bf16),
            pltpu.VMEM((kv_local, t * heads, group * HD), bf16),
            pltpu.VMEM((kv_local, heads, t, group * HD), bf16),
            pltpu.VMEM((heads,) + anchor_shape, bf16),
            pltpu.VMEM((heads,) + anchor_shape, bf16),
            pltpu.VMEM((levels + 1,) + anchor_shape, bf16),
            pltpu.VMEM((levels,) + anchor_shape, bf16),
            dma((heads,)), dma((heads,)), dma((levels,)), dma((levels,)),
            dma((kv_local, 2)), dma((kv_local, 2, heads)), dma((kv_local, 2, heads)),
            dma((kv_local,)), dma((kv_local, heads)), dma((kv_local, heads)),
            dma((kv_local, levels)), dma((kv_local, levels)),
            dma((kv_local,)), dma((kv_local, heads)), dma((kv_local, heads)),
        ],
        compiler_params=pltpu.CompilerParams(collective_id=0, has_side_effects=True),
        name="attend",
    )(bias, selector, keys, values, queries)


def solution(mesh):
    in_specs = (
        P(("seq", "head"), None),
        P(("seq", "head"), None),
        P(("seq", "head"), None),
        P("head", None),
        P("head"),
        P("seq", None),
        P(),
    )
    out_specs = P(("seq", "head"), None)
    return jax.shard_map(
        on_device, mesh=mesh, in_specs=in_specs, out_specs=out_specs, check_vma=False
    )
```

```python
import functools

import jax
import jax.numpy as jnp
from jax import lax
from jax.experimental import pallas as pl
from jax.experimental.pallas import tpu as pltpu
from jax.sharding import PartitionSpec as P

HD = 128
LOG2E = 1.4426950408889634


def attend(query, key_parts, value_parts, biases, scale):
    scores = [
        lax.dot_general(query, k, (((1,), (1,)), ((), ())), preferred_element_type=jnp.float32)
        for k in key_parts
    ]
    row_max = None
    for s, b in zip(scores, biases):
        top = jnp.max(s, axis=1, keepdims=True) * scale + b
        row_max = top if row_max is None else jnp.maximum(row_max, top)
    total = None
    acc = None
    for s, v, b in zip(scores, value_parts, biases):
        p = jnp.exp2(s * scale + (b - row_max))
        part = jnp.sum(p, axis=1, keepdims=True)
        out = jnp.dot(p.astype(jnp.bfloat16), v, preferred_element_type=jnp.float32)
        total = part if total is None else total + part
        acc = out if acc is None else acc + out
    return acc / total


def kernel(
    heads, levels, kv_local, group,
    level_ref, anchor_ref, partners_ref, places_ref, keys_ref, values_ref, queries_ref, out_ref,
    blocks, qbuf, obuf, part, part_in, carry, carry_in,
    part_send, part_recv, carry_send, carry_recv,
    own_sem, x_send, x_recv, own_q_sem, q_send, q_recv,
    lv_send, lv_recv, own_o_sem, o_send, o_recv,
):
    me = lax.axis_index("head")
    seat = lax.axis_index("seq")
    t = keys_ref.shape[0]
    wide = group * HD
    scale = HD ** -0.5 * LOG2E
    mesh_id = pl.DeviceIdType.MESH

    def peer(d):
        return lax.rem(me + d, heads)

    def partner(l):
        bit = lax.rem(lax.div(seat, 1 << l), 2)
        return seat + (1 - 2 * bit) * (1 << l)

    barrier = pltpu.get_barrier_semaphore()
    for d in range(1, heads):
        pl.semaphore_signal(barrier, inc=1, device_id={"head": peer(d)}, device_id_type=mesh_id)
    for l in range(levels):
        pl.semaphore_signal(barrier, inc=1, device_id={"seq": partner(l)}, device_id_type=mesh_id)

    def cols(owner, j, width):
        return pl.ds(pl.multiple_of((owner * kv_local + j) * width, width), width)

    def rows(owner):
        return pl.ds(pl.multiple_of(owner * t, t), t)

    def own_copy(j, c):
        src = (keys_ref, values_ref)[c]
        return pltpu.make_async_copy(
            src.at[:, cols(me, j, HD)], blocks.at[0, j, c, rows(me)], own_sem.at[j, c])

    def own_q(j):
        return pltpu.make_async_copy(
            queries_ref.at[:, cols(me, j, wide)], qbuf.at[j, rows(me)], own_q_sem.at[j])

    def send_kv(j, c, d):
        src = (keys_ref, values_ref)[c]
        return pltpu.make_async_remote_copy(
            src_ref=src.at[:, cols(peer(d), j, HD)], dst_ref=blocks.at[0, j, c, rows(me)],
            send_sem=x_send.at[j, c, d], recv_sem=x_recv.at[j, c, d],
            device_id={"head": peer(d)}, device_id_type=mesh_id)

    def came_kv(j, c, d):
        src = (keys_ref, values_ref)[c]
        return pltpu.make_async_remote_copy(
            src_ref=src.at[:, cols(me, j, HD)], dst_ref=blocks.at[0, j, c, rows(peer(heads - d))],
            send_sem=x_send.at[j, c, d], recv_sem=x_recv.at[j, c, d],
            device_id={"head": peer(d)}, device_id_type=mesh_id)

    def send_q(j, d):
        return pltpu.make_async_remote_copy(
            src_ref=queries_ref.at[:, cols(peer(d), j, wide)], dst_ref=qbuf.at[j, rows(me)],
            send_sem=q_send.at[j, d], recv_sem=q_recv.at[j, d],
            device_id={"head": peer(d)}, device_id_type=mesh_id)

    def came_q(j, d):
        return pltpu.make_async_remote_copy(
            src_ref=queries_ref.at[:, cols(me, j, wide)], dst_ref=qbuf.at[j, rows(peer(heads - d))],
            send_sem=q_send.at[j, d], recv_sem=q_recv.at[j, d],
            device_id={"head": peer(d)}, device_id_type=mesh_id)

    def send_level(j, l):
        return pltpu.make_async_remote_copy(
            src_ref=blocks.at[0, j], dst_ref=blocks.at[l + 1, j],
            send_sem=lv_send.at[j, l], recv_sem=lv_recv.at[j, l],
            device_id={"seq": partner(l)}, device_id_type=mesh_id)

    def send_part(d):
        return pltpu.make_async_remote_copy(
            src_ref=part.at[d], dst_ref=part_in.at[d],
            send_sem=part_send.at[d], recv_sem=part_recv.at[d],
            device_id={"head": peer(d)}, device_id_type=mesh_id)

    def send_carry(l):
        return pltpu.make_async_remote_copy(
            src_ref=carry.at[l + 1], dst_ref=carry_in.at[l],
            send_sem=carry_send.at[l], recv_sem=carry_recv.at[l],
            device_id={"seq": partner(l)}, device_id_type=mesh_id)

    def send_out(j, d):
        return pltpu.make_async_remote_copy(
            src_ref=obuf.at[j, d], dst_ref=out_ref.at[:, cols(me, j, wide)],
            send_sem=o_send.at[j, d], recv_sem=o_recv.at[j, d],
            device_id={"head": peer(d)}, device_id_type=mesh_id)

    def came_out(j, d):
        return pltpu.make_async_remote_copy(
            src_ref=obuf.at[j, d], dst_ref=out_ref.at[:, cols(peer(heads - d), j, wide)],
            send_sem=o_send.at[j, d], recv_sem=o_recv.at[j, d],
            device_id={"head": peer(d)}, device_id_type=mesh_id)

    def own_out(j):
        return pltpu.make_async_copy(
            obuf.at[j, 0], out_ref.at[:, cols(me, j, wide)], own_o_sem.at[j])

    for j in range(kv_local):
        for c in range(2):
            own_copy(j, c).start()
        own_q(j).start()
    first = (seat * heads + me) * t
    places = places_ref[...] - first
    token = lax.broadcasted_iota(jnp.int32, (places.shape[0], t), 1)
    selector = jnp.where(places == token, 1.0, 0.0).astype(jnp.bfloat16)
    for d in range(heads):
        for j in range(kv_local):
            for c in range(2):
                src = (keys_ref, values_ref)[c]
                part[d, j, c] = jnp.dot(
                    selector, src[:, cols(peer(d), j, HD)], preferred_element_type=jnp.float32
                ).astype(jnp.bfloat16)
    pl.semaphore_wait(barrier, heads - 1 + levels)
    for d in range(1, heads):
        send_part(d).start()
    for j in range(kv_local):
        for d in range(1, heads):
            for c in range(2):
                send_kv(j, c, d).start()
    for j in range(kv_local):
        for d in range(1, heads):
            send_q(j, d).start()

    def forward(j):
        for c in range(2):
            own_copy(j, c).wait()
            for d in range(1, heads):
                came_kv(j, c, d).wait_recv()
        for l in reversed(range(levels)):
            send_level(j, l).start()

    held = part[0].astype(jnp.float32)
    for d in range(1, heads):
        send_part(d).wait_recv()
        held = held + part_in[d].astype(jnp.float32)
    carry[levels] = held.astype(jnp.bfloat16)
    for l in reversed(range(levels)):
        send_carry(l).start()
        if levels - 1 - l < kv_local:
            forward(levels - 1 - l)
        send_carry(l).wait_recv()
        carry[l] = (carry[l + 1].astype(jnp.float32) + carry_in[l].astype(jnp.float32)).astype(
            jnp.bfloat16)
    for j in range(levels, kv_local):
        forward(j)

    def biases(h):
        found = [jnp.float32(0.0)]
        for l in range(levels):
            total = jnp.float32(0.0)
            for m in range(levels):
                total += jnp.where(partners_ref[0, m] == partner(l), level_ref[h, m], 0.0)
            found.append(total * LOG2E)
        return found + [anchor_ref[h] * LOG2E]

    def one(step, _):
        j = lax.div(step, heads)
        turn = lax.rem(step, heads)

        @pl.when(turn == 0)
        def _():
            own_q(j).wait()
            for d in range(1, heads):
                came_q(j, d).wait_recv()
            for l in range(levels):
                send_level(j, l).wait_recv()

        d = lax.rem(turn + 1, heads)
        here = rows(peer(d))
        for g in range(group):
            result = attend(
                qbuf[j, here, g * HD:(g + 1) * HD],
                [blocks[n, j, 0] for n in range(levels + 1)] + [carry[0, j, 0]],
                [blocks[n, j, 1] for n in range(levels + 1)] + [carry[0, j, 1]],
                biases(j * group + g),
                scale,
            )
            obuf[j, d, :, g * HD:(g + 1) * HD] = result.astype(jnp.bfloat16)

        @pl.when(turn < heads - 1)
        def _():
            send_out(j, d).start()

        @pl.when(turn == heads - 1)
        def _():
            own_out(j).start()

        return 0

    lax.fori_loop(0, kv_local * heads, one, 0)

    for d in range(1, heads):
        send_part(d).wait_send()
    for l in range(levels):
        send_carry(l).wait_send()
    for j in range(kv_local):
        own_out(j).wait()
        for l in range(levels):
            send_level(j, l).wait_send()
        for d in range(1, heads):
            for c in range(2):
                send_kv(j, c, d).wait_send()
            send_q(j, d).wait_send()
            send_out(j, d).wait_send()
            came_out(j, d).wait_recv()


def on_device(queries, keys, values, level_bias, anchor_bias, partners, anchor_positions):
    t = queries.shape[0]
    heads = lax.axis_size("head")
    levels = lax.axis_size("seq").bit_length() - 1
    kv_local = keys.shape[1] // HD // heads
    group = level_bias.shape[0] // kv_local
    anchors = anchor_positions.shape[0]
    smem = pl.BlockSpec(memory_space=pltpu.SMEM)
    vmem = pl.BlockSpec(memory_space=pltpu.VMEM)
    dma = pltpu.SemaphoreType.DMA
    anchor_shape = (kv_local, 2, anchors, HD)
    bf16 = jnp.bfloat16
    return pl.pallas_call(
        functools.partial(kernel, heads, levels, kv_local, group),
        in_specs=[smem, smem, smem, vmem, vmem, vmem,
                  pl.BlockSpec(memory_space=pl.ANY)],
        out_specs=pl.BlockSpec(memory_space=pl.ANY),
        out_shape=jax.ShapeDtypeStruct(queries.shape, queries.dtype),
        scratch_shapes=[
            pltpu.VMEM((levels + 1, kv_local, 2, t * heads, HD), bf16),
            pltpu.VMEM((kv_local, t * heads, group * HD), bf16),
            pltpu.VMEM((kv_local, heads, t, group * HD), bf16),
            pltpu.VMEM((heads,) + anchor_shape, bf16),
            pltpu.VMEM((heads,) + anchor_shape, bf16),
            pltpu.VMEM((levels + 1,) + anchor_shape, bf16),
            pltpu.VMEM((levels,) + anchor_shape, bf16),
            dma((heads,)), dma((heads,)), dma((levels,)), dma((levels,)),
            dma((kv_local, 2)), dma((kv_local, 2, heads)), dma((kv_local, 2, heads)),
            dma((kv_local,)), dma((kv_local, heads)), dma((kv_local, heads)),
            dma((kv_local, levels)), dma((kv_local, levels)),
            dma((kv_local,)), dma((kv_local, heads)), dma((kv_local, heads)),
        ],
        compiler_params=pltpu.CompilerParams(collective_id=0, has_side_effects=True),
        name="attend",
    )(level_bias, anchor_bias, partners, anchor_positions[:, None], keys, values, queries)


def solution(mesh):
    in_specs = (
        P(("seq", "head"), None),
        P(("seq", "head"), None),
        P(("seq", "head"), None),
        P("head", None),
        P("head"),
        P("seq", None),
        P(),
    )
    out_specs = P(("seq", "head"), None)
    return jax.shard_map(
        on_device, mesh=mesh, in_specs=in_specs, out_specs=out_specs, check_vma=False
    )
```
